32 devices in a mesh: seq: 8 (over z, y), pat: 4 (over x, core).
Axes of the slice: x: 2, y: 2, z: 4, core: 2. Of those that a mesh axis runs over, the one named last changes fastest.
Arguments:
- queries: bfloat16 [4, 2048, 2048], P('pat', 'seq'), may hold values from -6 to 6
- key_rows: bfloat16 [4, 2048, 2048], P('pat', 'seq'), may hold values from -6 to 6
- value_rows: bfloat16 [4, 2048, 2048], P('pat', 'seq'), may hold values from -6 to 6
- out_weight: bfloat16 [2048, 2048], P('pat'), may hold values from -0.125 to 0.125
- grad_out: bfloat16 [4, 2048, 2048], P('pat', 'seq'), may hold values from -6 to 6
- visit_mask: int32 [4, 8, 2, 2], P('pat', 'seq'), may hold values 0 or 1
- lengths: int32 [4], P('pat'), may hold values from 256 to 2048, as said below
Outputs:
- mixed: bfloat16 [4, 2048, 2048], P('pat', 'seq')
- query_grad: bfloat16 [4, 2048, 2048], P('pat', 'seq')
- key_grad: bfloat16 [4, 2048, 2048], P('pat', 'seq')
- value_grad: bfloat16 [4, 2048, 2048], P('pat', 'seq')
- weight_grad: float32 [2048, 2048], P('pat', 'seq')
The draws below stay inside these ranges and needn't reach their ends.
Inputs may be any that keep to these rules, and one draw needn't show every extreme that they name: `lengths`: one patient's record fills all 2048 positions in every draw.
All inputs are finite; a program needn't handle non-finite values. No bound on the sum of `visit_mask` on one device may be relied on, other than what follows from the above.
Results may differ from the reference program's by a relative error of at most 0.013.
Values may be sent and summed in bfloat16 or wider, within the bound.
A program may use at most 384 MiB of HBM per device.

```python
import math
import jax
import jax.numpy as jnp
from jax import lax

H = 16
HD = 128
D = 2048
TOK_DEV = 256
NB = 2
GROUPS = 8
LEN = 2048
PATS = 4
N_SEQ = 8


def draw_lengths(key, part):
    base_key, pick_key = jax.random.split(jax.random.fold_in(key, 7))
    drawn = jax.random.randint(base_key, (PATS,), LEN // 8, LEN + 1)
    chosen = jax.random.randint(pick_key, (), 0, PATS)
    return jnp.where(jnp.arange(PATS) == chosen, LEN, drawn).astype(jnp.int32)


def with_ends(values, rng, low, top_value):
    index_at = [jax.random.randint(jax.random.fold_in(rng, axis), (), 0, length) for axis, length in enumerate(values.shape)]
    widest = values.shape.index(max(values.shape))
    next_to = index_at[:widest] + [(index_at[widest] + 1) % values.shape[widest]] + index_at[widest + 1:]
    return values.at[tuple(index_at)].set(low).at[tuple(next_to)].set(top_value)


def with_spikes(values, stream_key, source, target, shards_of, factor):
    def block_of(axis_at):
        return (jnp.arange(values.shape[axis_at]) // (values.shape[axis_at] // shards_of)).reshape((-1,) + (1,) * (values.ndim - 1 - axis_at))

    one_side = jax.random.permutation(stream_key, shards_of)[block_of(target)]
    far = (block_of(target) + shards_of // 2) % shards_of
    return jnp.where((block_of(source) == one_side) | (block_of(source) == far), factor * values, values)


def steps_of(stream_key, dims, cuts, low, largest):
    level, own = 1.0, jax.random.fold_in(stream_key, 6)
    for position, blocks in cuts:
        draws = jnp.exp(jax.random.uniform(jax.random.fold_in(own, position), (blocks,), jnp.float32, low / len(cuts), largest / len(cuts)))
        level = level * jnp.repeat(draws, dims[position] // blocks).reshape([-1 if axis == position else 1 for axis in range(len(dims))])
    return level


def centred(key, shape, scale, limit, cuts=(), held_as=jnp.bfloat16):
    values = scale * jax.random.normal(key, shape, jnp.float32)
    if cuts:
        values = values * steps_of(key, shape, cuts, -0.22, 0.18)
    return jnp.clip(values, -limit, limit).astype(held_as)


def bell_draw_with(own_key, extent, deviation, limit, shards, heavy, kind=jnp.bfloat16):
    values = deviation * jax.random.normal(own_key, extent, jnp.float32)
    if shards:
        values = values * steps_of(own_key, extent, shards, -0.22, 0.18)
    return jnp.clip(with_spikes(values, jax.random.fold_in(own_key, 3), *heavy), -limit, limit).astype(kind)


def setup_inputs(seed: int = 0) -> dict:
    splits = jax.random.split(jax.random.key(seed), 8)
    queries = centred(splits[0], (PATS, LEN, D), 1.0, 6.0, ((0, 4), (1, 8)))
    key_rows = centred(splits[1], (PATS, LEN, D), 1.0, 6.0, ((0, 4), (1, 8)))
    value_rows = centred(splits[2], (PATS, LEN, D), 1.0, 6.0, ((0, 4), (1, 8)))
    out_weight = centred(splits[3], (D, D), D ** -0.5, 0.125, ((0, 4),))
    grad_out = bell_draw_with(splits[4], (PATS, LEN, D), 1.0, 6.0, ((0, 4), (1, 8)), (1, 2, 8, 2.0))
    visit_mask = with_ends((jax.random.randint(splits[5], (PATS, GROUPS, NB, NB), 0, 2) < 1).astype(jnp.int32), jax.random.fold_in(splits[5], 1), 0, 1)
    lengths = draw_lengths(jax.random.fold_in(splits[7], 71), 0)
    return {"queries": queries, "key_rows": key_rows, "value_rows": value_rows, "out_weight": out_weight, "grad_out": grad_out, "visit_mask": visit_mask, "lengths": lengths}


def pair_mask(block_mask, live_mask, row_count):
    block_count = block_mask.shape[0]
    block_rows = row_count // block_count
    block_grid = jnp.repeat(jnp.repeat(block_mask, block_rows, axis=0), block_rows, axis=1)
    row_index = jnp.arange(row_count, dtype=jnp.int32)
    same_block = row_index[:, None] // block_rows == row_index[None, :] // block_rows
    causal = row_index[:, None] >= row_index[None, :]
    keep_mask = causal & (same_block | (block_grid == 1))
    return keep_mask.astype(jnp.float32) * live_mask[:, None] * live_mask[None, :]

def group_pass(query_rows, key_rows, value_rows, scaled_grad, live_mask, row_scale, allowed, state_before, state_after):
    head_count = state_before.shape[0]
    head_dim = state_before.shape[1]
    row_count = query_rows.shape[0]
    query_heads = query_rows.reshape(row_count, head_count, head_dim)
    key_heads = key_rows.reshape(row_count, head_count, head_dim)
    value_heads = value_rows.reshape(row_count, head_count, head_dim)
    grad_heads = scaled_grad.reshape(row_count, head_count, head_dim)
    highest = lax.Precision.HIGHEST
    scores = jnp.einsum('thd,shd->hts', query_heads, key_heads, preferred_element_type=jnp.float32) * allowed[None]
    score_half = scores.astype(jnp.bfloat16)
    within = jnp.einsum('hts,she->the', score_half, value_heads, preferred_element_type=jnp.float32)
    carried = jnp.einsum('thd,hde->the', query_heads.astype(jnp.float32), state_before, precision=highest)
    attended = (row_scale[:, None, None] * (within + carried)).reshape(row_count, -1).astype(jnp.bfloat16)
    grad_scores = jnp.einsum('the,she->hts', grad_heads, value_heads, preferred_element_type=jnp.float32) * allowed[None]
    grad_half = grad_scores.astype(jnp.bfloat16)
    query_grad = jnp.einsum('hts,shd->thd', grad_half, key_heads, preferred_element_type=jnp.float32)
    query_grad = query_grad + jnp.einsum('the,hde->thd', grad_heads.astype(jnp.float32), state_before, precision=highest)
    key_grad = jnp.einsum('hts,thd->shd', grad_half, query_heads, preferred_element_type=jnp.float32)
    key_grad = key_grad + live_mask[:, None, None] * jnp.einsum('she,hde->shd', value_heads.astype(jnp.float32), state_after, precision=highest)
    value_grad = jnp.einsum('hts,the->she', score_half, grad_heads, preferred_element_type=jnp.float32)
    value_grad = value_grad + live_mask[:, None, None] * jnp.einsum('shd,hde->she', key_heads.astype(jnp.float32), state_after, precision=highest)
    return (attended, query_grad.reshape(row_count, -1).astype(jnp.bfloat16), key_grad.reshape(row_count, -1).astype(jnp.bfloat16), value_grad.reshape(row_count, -1).astype(jnp.bfloat16))

def reference(queries, key_rows, value_rows, out_weight, grad_out, visit_mask, lengths):
    group_total = N_SEQ
    row_count = TOK_DEV
    flat_grad = grad_out.reshape(PATS * LEN, D)
    grad_attended = lax.dot_general(flat_grad, out_weight, (((1,), (1,)), ((), ())), preferred_element_type=jnp.float32).astype(jnp.bfloat16)
    grad_attended = grad_attended.reshape(PATS, group_total, row_count, D)

    def one_patient(inputs):
        query_p, key_p, value_p, grad_p, mask_p, length = inputs
        query_c = query_p.reshape(group_total, row_count, D)
        key_c = key_p.reshape(group_total, row_count, D)
        value_c = value_p.reshape(group_total, row_count, D)
        positions = jnp.arange(LEN, dtype=jnp.int32).reshape(group_total, row_count)
        live_mask = (positions < length).astype(jnp.float32)
        row_scale = live_mask * lax.rsqrt((positions + 1).astype(jnp.float32)) / math.sqrt(HD)
        scaled_grad = (row_scale[:, :, None] * grad_p.astype(jnp.float32)).astype(jnp.bfloat16)
        kept_keys = (key_c * live_mask[:, :, None].astype(jnp.bfloat16)).reshape(group_total, row_count, H, HD)
        state_local = jnp.einsum('cshd,cshe->chde', kept_keys, value_c.reshape(group_total, row_count, H, HD), preferred_element_type=jnp.float32)
        reverse_local = jnp.einsum('cthd,cthe->chde', query_c.reshape(group_total, row_count, H, HD), scaled_grad.reshape(group_total, row_count, H, HD), preferred_element_type=jnp.float32)
        zero_state = jnp.zeros((1, H, HD, HD), jnp.float32)
        state_before = jnp.concatenate([zero_state, jnp.cumsum(state_local, axis=0)[:-1]], axis=0)
        suffix_sums = jnp.cumsum(reverse_local[::-1], axis=0)[::-1]
        state_after = jnp.concatenate([suffix_sums[1:], zero_state], axis=0)

        def one_group(pieces):
            q_rows, k_rows, v_rows, g_rows, block_mask, live_c, scale_c, before_c, after_c = pieces
            allowed = pair_mask(block_mask, live_c, row_count)
            return group_pass(q_rows, k_rows, v_rows, g_rows, live_c, scale_c, allowed, before_c, after_c)
        return lax.map(one_group, (query_c, key_c, value_c, scaled_grad, mask_p, live_mask, row_scale, state_before, state_after))
    attended, query_grad, key_grad, value_grad = lax.map(one_patient, (queries, key_rows, value_rows, grad_attended, visit_mask, lengths))
    flat_attended = attended.reshape(PATS * LEN, D)
    mixed = jnp.dot(flat_attended, out_weight, preferred_element_type=jnp.float32).astype(jnp.bfloat16)
    weight_grad = lax.dot_general(flat_attended, flat_grad, (((0,), (0,)), ((), ())), preferred_element_type=jnp.float32) / math.sqrt(PATS * LEN)
    shape = (PATS, LEN, D)
    return (mixed.reshape(shape), query_grad.reshape(shape), key_grad.reshape(shape), value_grad.reshape(shape), weight_grad)
```

```python
import math

import jax
import jax.numpy as jnp
from jax import lax
from jax.experimental import pallas as pl
from jax.experimental.pallas import tpu as pltpu
from jax.sharding import PartitionSpec as P

HD = 128
NW = 8
NSC = 4
MESH = pl.DeviceIdType.MESH
F32 = jnp.float32
BF = jnp.bfloat16


def dot(a, b, ca, cb):
    return lax.dot_general(a, b, (((ca,), (cb,)), ((), ())), preferred_element_type=F32)


def make_kernel(n, np_, rows, width, nb, grad_scale):
    heads = width // HD
    per = heads // np_
    blk = per * HD
    piece = width // n
    m = n // 2
    pairs = np_ // 2
    half_rows = heads * HD // 2
    crows = half_rows // NSC
    wrows = blk // NW
    gcols = 256
    gcount = width // (2 * gcols)

    def kernel(
        q, k, v, go, w, vm, ln,
        mixed, dq, dk, dv, wg,
        w_all, go_all, att, attc, att_t, sc, gi, allowed, g, dk0, dv0,
        st, sb, rv, sa,
        pf, nf, of, yf, pb_, nb_, ob, yb,
        part, pbox, zpart,
        lsem, ps, pr, ys, yr, zs, zr, cs, cr,
    ):
        me = lax.axis_index("pat")
        si = lax.axis_index("seq")
        sib = me + 1 - 2 * (me % 2)
        xp = (me + 2) % np_
        diag = (sib + 2) % np_
        cx = me // 2
        yi = si % 2
        zi = si // 2
        yo = 1 - yi
        zb = zi % 2
        partner = si + 1 - 2 * yi

        def zpeer(d):
            return ((zi + d) % m) * 2 + yi

        barrier = pltpu.get_barrier_semaphore()
        for peer in (sib, xp, diag):
            pl.semaphore_signal(barrier, inc=1, device_id={"pat": peer}, device_id_type=MESH)
        for peer in [partner] + [zpeer(d) for d in range(1, m)]:
            pl.semaphore_signal(barrier, inc=1, device_id={"seq": peer}, device_id_type=MESH)
        pl.semaphore_wait(barrier, 3 + m)

        n_pat = [0]
        n_y = [0]
        n_z = [0]

        def pat_copy(src, dst, peer):
            i = n_pat[0]
            n_pat[0] += 1
            return pltpu.make_async_remote_copy(
                src_ref=src, dst_ref=dst, send_sem=ps.at[i], recv_sem=pr.at[i],
                device_id={"pat": peer}, device_id_type=MESH,
            )

        def y_copy(src, dst):
            i = n_y[0]
            n_y[0] += 1
            return pltpu.make_async_remote_copy(
                src_ref=src, dst_ref=dst, send_sem=ys.at[i], recv_sem=yr.at[i],
                device_id={"seq": partner}, device_id_type=MESH,
            )

        def z_copy(src, dst, peer):
            i = n_z[0]
            n_z[0] += 1
            return pltpu.make_async_remote_copy(
                src_ref=src, dst_ref=dst, send_sem=zs.at[i], recv_sem=zr.at[i],
                device_id={"seq": peer}, device_id_type=MESH,
            )

        def wsl(c):
            return pl.ds(pl.multiple_of(c * wrows, wrows), wrows)

        local_w = pltpu.make_async_copy(w, w_all.at[me], lsem.at[0])
        local_go = pltpu.make_async_copy(go, go_all.at[me], lsem.at[1])
        w_sib = pat_copy(w, w_all.at[me], sib)
        go_sib = pat_copy(go, go_all.at[me], sib)

        zpair = (zi + 1 - 2 * zb) * 2 + yi
        x_set = [wsl(4 + 2 * yi + zb), wsl(2 * zb), wsl(2 * zb + 1)]
        z_set = [wsl(5 + 2 * yi - zb), wsl(2 - 2 * zb), wsl(3 - 2 * zb)]
        y_set = [wsl(4 + 2 * yo + zb), wsl(5 + 2 * yo - zb)]
        w_x = [pat_copy(w.at[s], w_all.at[me, s], xp) for s in x_set]
        w_z = [z_copy(w_all.at[xp, s], w_all.at[xp, s], zpair) for s in x_set]
        w_y = [y_copy(w_all.at[xp, s], w_all.at[xp, s]) for s in (x_set[0], z_set[0])]
        relay = {}
        for name, group in (("x", x_set), ("z", z_set), ("y", y_set)):
            relay[name] = [pat_copy(w_all.at[xp, s], w_all.at[xp, s], sib) for s in group]

        def gsl(t, odd):
            return pl.ds(pl.multiple_of((2 * t + odd) * gcols, gcols), gcols)

        g_x, g_relay = [], []
        for odd in (yo, yi):
            cols = [gsl(t, odd) for t in range(gcount)]
            g_x.append([pat_copy(go.at[:, c], go_all.at[me, :, c], xp) for c in cols])
            g_relay.append([pat_copy(go_all.at[xp, :, c], go_all.at[xp, :, c], sib) for c in cols])
        att_out = [pat_copy(att.at[peer], attc.at[me], peer) for peer in (xp, diag, sib)]

        for copy in w_x:
            copy.start()
        w_sib.start()
        local_w.start()
        go_sib.start()
        local_go.start()
        for copy in g_x[0]:
            copy.start()

        pos_c = si * rows + lax.broadcasted_iota(jnp.int32, (rows, 1), 0)
        pos_r = si * rows + lax.broadcasted_iota(jnp.int32, (1, rows), 1)
        live = jnp.where(pos_c < ln[0], 1.0, 0.0).astype(F32)
        live_r = jnp.where(pos_r < ln[0], 1.0, 0.0).astype(F32)
        live_h = live.astype(BF)
        scale = live * lax.rsqrt((pos_c + 1).astype(F32)) / math.sqrt(HD)

        def wait(copies):
            for copy in copies:
                copy.wait()

        def lanes(pb, i, size=HD):
            return pl.ds(pl.multiple_of(pb * blk + i * HD, HD), size)

        near, far = cx, 1 - cx

        def each_block(side, body):
            @pl.loop(0, pairs)
            def _(t):
                body(side * pairs + t)

        class Scan:
            def __init__(self, own, dst, before, ahead, out, box, base, forward):
                self.own, self.dst, self.before, self.ahead = own, dst, before, ahead
                self.out, self.box, self.base, self.forward = out, box, base, forward
                step = 1 if forward else m - 1
                self.peer = zpeer(step)
                self.first = zi == (0 if forward else m - 1)
                self.last = zi == (m - 1 if forward else 0)
                self.give = (yo if forward else yi).astype(F32)

                @pl.when(self.first)
                def _():
                    self.before[...] = jnp.zeros_like(self.before)

            def at(self, side, c):
                return pl.ds(pl.multiple_of(side * half_rows + c * crows, crows), crows)

            def z(self, side, order, c):
                i = self.base + order * NSC + c
                spot = self.at(side, c)
                return pltpu.make_async_remote_copy(
                    src_ref=self.ahead.at[spot], dst_ref=self.before.at[spot],
                    send_sem=cs.at[0, i], recv_sem=cr.at[0, i],
                    device_id={"seq": self.peer}, device_id_type=MESH,
                )

            def y(self, side, order, c):
                i = self.base + order * NSC + c
                spot = self.at(side, c)
                return pltpu.make_async_remote_copy(
                    src_ref=self.out.at[spot], dst_ref=self.box.at[spot],
                    send_sem=cs.at[1, i], recv_sem=cr.at[1, i],
                    device_id={"seq": partner}, device_id_type=MESH,
                )

            def serve(self, side, order):
                @pl.loop(0, NSC)
                def _(c):
                    spot = self.at(side, c)
                    z = self.z(side, order, c)

                    @pl.when(jnp.logical_not(self.first))
                    def _():
                        z.wait_recv()

                    had = self.before[spot, :].astype(F32)
                    own = self.own[spot, :].astype(F32)
                    self.ahead[spot, :] = (had + own).astype(BF)

                    @pl.when(jnp.logical_not(self.last))
                    def _():
                        z.start()

                    self.out[spot, :] = (had + self.give * own).astype(BF)
                    self.y(side, order, c).start()

            def finish(self, side, order):
                @pl.loop(0, NSC)
                def _(c):
                    spot = self.at(side, c)
                    self.y(side, order, c).wait()

                    @pl.when(jnp.logical_not(self.last))
                    def _():
                        self.z(side, order, c).wait_send()

                    total = self.before[spot, :].astype(F32) + self.box[spot, :].astype(F32)
                    self.dst[spot, :] = total.astype(BF)

        fwd = Scan(st, sb, pf, nf, of, yf, 0, True)
        bwd = Scan(rv, sa, pb_, nb_, ob, yb, 2 * NSC, False)

        def states(pb):
            for i in range(per):
                ls = lanes(pb, i)
                st[ls, :] = dot(k[:, ls] * live_h, v[:, ls], 0, 0).astype(BF)

        def scores(pb):
            for i in range(per):
                ls = lanes(pb, i)
                s = dot(q[:, ls], k[:, ls], 1, 1) * allowed[...]
                sc[pb * per + i] = s.astype(BF)

        def attend(pb):
            for i in range(per):
                ls = lanes(pb, i)
                inner = dot(sc[pb * per + i], v[:, ls], 1, 0) + dot(q[:, ls], sb[ls, :], 1, 0)
                att[pb, :, i * HD : (i + 1) * HD] = (scale * inner).astype(BF)

        def grad_block(pb):
            @pl.loop(0, blk // 256)
            def _(c):
                at = pl.ds(pl.multiple_of(c * 256, 256), 256)
                ga = dot(go[...], w_all[pb, at, :], 1, 1).astype(BF)
                gg = (scale * ga.astype(F32)).astype(BF)
                g[:, pl.ds(pl.multiple_of(pb * blk + c * 256, HD), 256)] = gg
                for i in range(256 // HD):
                    ls = pl.ds(pl.multiple_of(pb * blk + c * 256 + i * HD, HD), HD)
                    rv[ls, :] = dot(q[:, ls], gg[:, i * HD : (i + 1) * HD], 0, 0).astype(BF)

        def grads_within(pb):
            for i in range(per):
                ls = lanes(pb, i)
                gh = g[:, ls]
                inner = (dot(gh, v[:, ls], 1, 1) * allowed[...]).astype(BF)
                gi[pb * per + i] = inner
                dk0[:, ls] = dot(inner, q[:, ls], 0, 0)
                dv0[:, ls] = dot(sc[pb * per + i], gh, 0, 0)

        def grads_query(pb):
            for i in range(per):
                ls = lanes(pb, i)
                inner = gi[pb * per + i]
                dq[:, ls] = (dot(inner, k[:, ls], 1, 0) + dot(g[:, ls], sb[ls, :], 1, 1)).astype(BF)

        def finals(pb):
            for i in range(per):
                ls = lanes(pb, i)
                dk[:, ls] = (dk0[:, ls] + live * dot(v[:, ls], sa[ls, :], 1, 1)).astype(BF)
                dv[:, ls] = (dv0[:, ls] + live * dot(k[:, ls], sa[ls, :], 1, 0)).astype(BF)

        low = zi < m // 2
        high = zi >= m // 2

        each_block(far, states)

        @pl.when(fwd.first)
        def _():
            fwd.serve(far, 0)

        each_block(near, states)

        @pl.when(fwd.first)
        def _():
            fwd.serve(near, 1)

        local_w.wait()
        grad_block(me)
        w_sib.wait()
        grad_block(sib)

        @pl.when(bwd.first)
        def _():
            bwd.serve(near, 0)

        row_i = lax.broadcasted_iota(jnp.int32, (rows, rows), 0)
        col_i = lax.broadcasted_iota(jnp.int32, (rows, rows), 1)
        rb, cb = row_i // (rows // nb), col_i // (rows // nb)
        keep = jnp.where(rb == cb, 1.0, 0.0).astype(F32)
        for i in range(nb):
            for j in range(i):
                on = jnp.where(vm[0, 0, i, j] == 1, 1.0, 0.0).astype(F32)
                keep = keep + jnp.where((rb == i) & (cb == j), on, 0.0)
        allowed[...] = jnp.where(row_i >= col_i, keep, 0.0) * live * live_r

        each_block(far, scores)

        w_x[0].wait()
        w_z[0].start()
        w_y[0].start()
        relay["x"][0].start()

        @pl.when(low & jnp.logical_not(fwd.first))
        def _():
            fwd.serve(far, 0)

        @pl.when(high & jnp.logical_not(bwd.first))
        def _():
            bwd.serve(near, 0)

        each_block(near, scores)
        w_x[1].wait()
        w_z[1].start()
        relay["x"][1].start()

        @pl.when(low & jnp.logical_not(fwd.first))
        def _():
            fwd.serve(near, 1)

        each_block(near, grads_within)

        @pl.when(high)
        def _():
            fwd.serve(far, 0)

        @pl.when(low)
        def _():
            bwd.serve(near, 0)

        w_x[2].wait()
        w_z[2].start()
        relay["x"][2].start()
        w_z[0].wait()
        w_y[1].start()
        relay["z"][0].start()

        fwd.finish(far, 0)
        each_block(far, attend)
        att_out[0].start()
        att_out[1].start()
        for copy in g_x[1]:
            copy.start()

        @pl.when(high)
        def _():
            fwd.serve(near, 1)

        w_y[0].wait()
        relay["y"][0].start()
        w_z[1].wait()
        relay["z"][1].start()
        fwd.finish(near, 1)
        each_block(near, attend)
        att_out[2].start()
        w_z[2].wait()
        relay["z"][2].start()
        w_y[1].wait()
        relay["y"][1].start()
        grad_block(xp)
        for name in ("x", "z", "y"):
            wait(relay[name])
        grad_block(diag)

        @pl.when(bwd.first)
        def _():
            bwd.serve(far, 1)

        local_go.wait()
        go_sib.wait()
        wait(g_x[0])
        for copy in g_relay[0]:
            copy.start()
        att_t[me] = att[me].T
        att_out[2].wait()
        att_t[sib] = attc[sib].T
        att_out[0].wait()
        att_t[xp] = attc[xp].T
        att_out[1].wait()
        att_t[diag] = attc[diag].T
        wait(g_relay[0])

        def product(cols):
            acc = dot(att_t[0], go_all[0, :, cols], 1, 0)
            for b in range(1, np_):
                acc = acc + dot(att_t[b], go_all[b, :, cols], 1, 0)
            return acc

        def cols_of(i):
            return pl.ds(pl.multiple_of(i * piece, HD), piece)

        def second_half():
            wait(g_x[1])
            for copy in g_relay[1]:
                copy.start()
            wait(g_relay[1])

        order = sorted(range(1, m), key=lambda d: -min(d, m - d)) + [m]
        if piece != gcols:
            second_half()
            for j in range(width // 256):
                acc = product(slice(j * 256, (j + 1) * 256))
                for i in range(256 // piece):
                    part[j * (256 // piece) + i] = acc[:, i * piece : (i + 1) * piece].astype(BF)
        y_out = {}
        for d in order:
            to = (zi + d) % m
            if piece == gcols:
                part[to * 2 + yo] = product(cols_of(to * 2 + yo)).astype(BF)
            y_out[d] = y_copy(part.at[to * 2 + yo], pbox.at[to])
            y_out[d].start()

        @pl.when(high & jnp.logical_not(bwd.first))
        def _():
            bwd.serve(far, 1)

        each_block(far, grads_within)

        @pl.when(low & jnp.logical_not(bwd.last))
        def _():
            bwd.serve(far, 1)

        bwd.finish(near, 0)
        each_block(near, grads_query)
        each_block(far, grads_query)

        @pl.when(bwd.last)
        def _():
            bwd.serve(far, 1)

        if piece == gcols:
            second_half()
        z_out = []
        for d in order:
            to = (zi + d) % m
            if piece == gcols:
                acc = product(cols_of(to * 2 + yi))
            else:
                acc = part[to * 2 + yi].astype(F32)
            y_out[d].wait()
            acc = acc + pbox[to].astype(F32)
            mine = to * 2 + yi
            part[mine] = acc.astype(BF)
            if d < m:
                copy = z_copy(part.at[mine], zpart.at[d], zpeer(d))
                copy.start()
                z_out.append(copy)
            else:
                zpart[0] = part[mine]

        @pl.loop(0, width // 256)
        def _(j):
            cols = pl.ds(pl.multiple_of(j * 256, 256), 256)
            acc = dot(att[0], w_all[0, :, cols], 1, 0)
            for b in range(1, np_):
                acc = acc + dot(att[b], w_all[b, :, cols], 1, 0)
            mixed[:, cols] = acc.astype(BF)

        each_block(near, finals)
        bwd.finish(far, 1)
        each_block(far, finals)

        wait(z_out)
        total = zpart[0].astype(F32)
        for s in range(1, m):
            total = total + zpart[s].astype(F32)
        wg[...] = total * grad_scale

    vmem = pltpu.VMEM
    sems = pltpu.SemaphoreType.DMA
    state = vmem((heads * HD, HD), BF)
    n_pat = 2 + 3 + NW + 4 * gcount + 3
    n_y = 2 + m
    n_z = 3 + m
    scratch = [
        vmem((np_, blk, width), BF),
        vmem((np_, rows, width), BF),
        vmem((np_, rows, blk), BF),
        vmem((np_, rows, blk), BF),
        vmem((np_, blk, rows), BF),
        vmem((heads, rows, rows), BF),
        vmem((heads, rows, rows), BF),
        vmem((rows, rows), F32),
        vmem((rows, width), BF),
        vmem((rows, width), F32),
        vmem((rows, width), F32),
        *[state] * 4,
        *[state] * 8,
        vmem((n, blk, piece), BF),
        vmem((m, blk, piece), BF),
        vmem((m, blk, piece), BF),
        sems((2,)),
        sems((n_pat,)), sems((n_pat,)),
        sems((n_y,)), sems((n_y,)),
        sems((n_z,)), sems((n_z,)),
        sems((2, 4 * NSC)), sems((2, 4 * NSC)),
    ]
    full = jax.ShapeDtypeStruct((rows, width), BF)
    whole = pl.BlockSpec(memory_space=pltpu.VMEM)
    scalar = pl.BlockSpec(memory_space=pltpu.SMEM)
    return pl.pallas_call(
        kernel,
        out_shape=(full, full, full, full, jax.ShapeDtypeStruct((blk, piece), F32)),
        in_specs=[whole] * 5 + [scalar] * 2,
        out_specs=(whole,) * 5,
        scratch_shapes=scratch,
        compiler_params=pltpu.CompilerParams(
            collective_id=0, has_side_effects=True, vmem_limit_bytes=60 * 1024 * 1024
        ),
    )


def solution(mesh):
    n, np_ = mesh.shape["seq"], mesh.shape["pat"]

    def on_device(queries, key_rows, value_rows, out_weight, grad_out, visit_mask, lengths):
        rows, width = queries.shape[1:]
        call = make_kernel(
            n, np_, rows, width, visit_mask.shape[-1], 1.0 / math.sqrt(np_ * n * rows)
        )
        mixed, dq, dk, dv, wg = call(
            queries[0], key_rows[0], value_rows[0], grad_out[0], out_weight, visit_mask, lengths
        )
        return mixed[None], dq[None], dk[None], dv[None], wg

    rows3 = P("pat", "seq", None)
    return jax.shard_map(
        on_device,
        mesh=mesh,
        in_specs=(rows3, rows3, rows3, P("pat", None), rows3, P("pat", "seq", None, None), P("pat")),
        out_specs=(rows3, rows3, rows3, rows3, P("pat", "seq")),
        check_vma=False,
    )
```

```python
import math

import jax
import jax.numpy as jnp
from jax import lax
from jax.experimental import pallas as pl
from jax.experimental.pallas import tpu as pltpu
from jax.sharding import PartitionSpec as P

HD = 128
NW = 8
NSC = 4
MESH = pl.DeviceIdType.MESH
F32 = jnp.float32
BF = jnp.bfloat16


def dot(a, b, ca, cb):
    return lax.dot_general(a, b, (((ca,), (cb,)), ((), ())), preferred_element_type=F32)


def make_kernel(n, np_, rows, width, nb, grad_scale):
    heads = width // HD
    per = heads // np_
    blk = per * HD
    piece = width // n
    m = n // 2
    pairs = np_ // 2
    half_rows = heads * HD // 2
    crows = half_rows // NSC
    wrows = blk // NW
    gcols = 256
    gcount = width // (2 * gcols)
    turns = blk // gcols

    def kernel(
        q_hbm, k_hbm, v_hbm, go, w, vm, ln,
        mixed, dq, dk, dv, wg,
        q, k, v, go_t, w_all, go_all, att, attc, att_t, sc, gi, allowed, g, dk0, dv0,
        st, sb, rv, sa,
        pf, nf, of, yf, pb_, nb_, ob, yb,
        part, pbox, zpart,
        lsem, ps, pr, ys, yr, zs, zr, cs, cr,
    ):
        me = lax.axis_index("pat")
        si = lax.axis_index("seq")
        sib = me + 1 - 2 * (me % 2)
        xp = (me + 2) % np_
        diag = (sib + 2) % np_
        cx = me // 2
        yi = si % 2
        zi = si // 2
        yo = 1 - yi
        zb = zi % 2
        partner = si + 1 - 2 * yi

        def zpeer(d):
            return ((zi + d) % m) * 2 + yi

        def wrow(p):
            return pl.ds(pl.multiple_of(p * blk, blk), blk)

        def grow(p):
            return pl.ds(pl.multiple_of(p * rows, rows), rows)

        loads = [
            pltpu.make_async_copy(a, b, lsem.at[i])
            for i, (a, b) in enumerate(
                ((k_hbm, k), (v_hbm, v), (q_hbm, q), (go, go_all.at[grow(me)]), (w, w_all.at[wrow(me)]))
            )
        ]
        for copy in loads:
            copy.start()
        barrier = pltpu.get_barrier_semaphore()
        for peer in (sib, xp, diag):
            pl.semaphore_signal(barrier, inc=1, device_id={"pat": peer}, device_id_type=MESH)
        for peer in [partner] + [zpeer(d) for d in range(1, m)]:
            pl.semaphore_signal(barrier, inc=1, device_id={"seq": peer}, device_id_type=MESH)
        pl.semaphore_wait(barrier, 3 + m)

        n_pat = [0]
        n_y = [0]
        n_z = [0]

        def pat_copy(src, dst, peer):
            i = n_pat[0]
            n_pat[0] += 1
            return pltpu.make_async_remote_copy(
                src_ref=src, dst_ref=dst, send_sem=ps.at[i], recv_sem=pr.at[i],
                device_id={"pat": peer}, device_id_type=MESH,
            )

        def y_copy(src, dst):
            i = n_y[0]
            n_y[0] += 1
            return pltpu.make_async_remote_copy(
                src_ref=src, dst_ref=dst, send_sem=ys.at[i], recv_sem=yr.at[i],
                device_id={"seq": partner}, device_id_type=MESH,
            )

        def z_copy(src, dst, peer):
            i = n_z[0]
            n_z[0] += 1
            return pltpu.make_async_remote_copy(
                src_ref=src, dst_ref=dst, send_sem=zs.at[i], recv_sem=zr.at[i],
                device_id={"seq": peer}, device_id_type=MESH,
            )

        def wsl(c, p=0):
            return pl.ds(pl.multiple_of(p * blk + c * wrows, wrows), wrows)

        w_sib = pat_copy(w, w_all.at[wrow(me)], sib)
        go_sib = pat_copy(go, go_all.at[grow(me)], sib)

        zpair = (zi + 1 - 2 * zb) * 2 + yi
        x_set = [4 + 2 * yi + zb, 2 * zb, 2 * zb + 1]
        z_set = [5 + 2 * yi - zb, 2 - 2 * zb, 3 - 2 * zb]
        y_set = [4 + 2 * yo + zb, 5 + 2 * yo - zb]

        def far_w(c):
            return w_all.at[wsl(c, xp)]

        w_x = [pat_copy(w.at[wsl(c)], w_all.at[wsl(c, me)], xp) for c in x_set]
        w_z = [z_copy(far_w(c), far_w(c), zpair) for c in x_set]
        w_y = [y_copy(far_w(c), far_w(c)) for c in (x_set[0], z_set[0])]
        relay = {}
        for name, group in (("x", x_set), ("z", z_set), ("y", y_set)):
            relay[name] = [pat_copy(far_w(c), far_w(c), sib) for c in group]

        def gsl(t, odd):
            return pl.ds(pl.multiple_of((2 * t + odd) * gcols, gcols), gcols)

        g_x, g_relay = [], []
        for odd in (yo, yi):
            cols = [gsl(t, odd) for t in range(gcount)]
            g_x.append([pat_copy(go.at[:, c], go_all.at[grow(me), c], xp) for c in cols])
            g_relay.append([pat_copy(go_all.at[grow(xp), c], go_all.at[grow(xp), c], sib) for c in cols])
        spans = [slice(r * gcols, (r + 1) * gcols) for r in range(turns)]

        def span(r):
            return pl.ds(r * gcols, gcols)

        def acol(p, r):
            return pl.ds(pl.multiple_of(p * blk + r * gcols, gcols), gcols)

        att_out = [
            [pat_copy(att.at[:, acol(p, r)], attc.at[me, :, spans[r]], p) for p in (xp, diag, sib)]
            for r in range(turns)
        ]

        for copy in w_x:
            copy.start()
        w_sib.start()
        go_sib.start()
        for copy in g_x[0]:
            copy.start()

        pos_c = si * rows + lax.broadcasted_iota(jnp.int32, (rows, 1), 0)
        pos_r = si * rows + lax.broadcasted_iota(jnp.int32, (1, rows), 1)
        live = jnp.where(pos_c < ln[0], 1.0, 0.0).astype(F32)
        live_r = jnp.where(pos_r < ln[0], 1.0, 0.0).astype(F32)
        live_h = live.astype(BF)
        scale = live * lax.rsqrt((pos_c + 1).astype(F32)) / math.sqrt(HD)

        def wait(copies):
            for copy in copies:
                copy.wait()

        def lanes(pb, i, size=HD):
            return pl.ds(pl.multiple_of(pb * blk + i * HD, HD), size)

        near, far = cx, 1 - cx

        def each_block(side, body):
            @pl.loop(0, pairs)
            def _(t):
                body(side * pairs + t)

        class Scan:
            def __init__(self, own, dst, before, ahead, out, box, base, forward):
                self.own, self.dst, self.before, self.ahead = own, dst, before, ahead
                self.out, self.box, self.base, self.forward = out, box, base, forward
                step = 1 if forward else m - 1
                self.peer = zpeer(step)
                self.first = zi == (0 if forward else m - 1)
                self.last = zi == (m - 1 if forward else 0)
                self.give = (yo if forward else yi).astype(F32)

                @pl.when(self.first)
                def _():
                    self.before[...] = jnp.zeros_like(self.before)

            def at(self, side, c):
                return pl.ds(pl.multiple_of(side * half_rows + c * crows, crows), crows)

            def z(self, side, order, c):
                i = self.base + order * NSC + c
                spot = self.at(side, c)
                return pltpu.make_async_remote_copy(
                    src_ref=self.ahead.at[spot], dst_ref=self.before.at[spot],
                    send_sem=cs.at[0, i], recv_sem=cr.at[0, i],
                    device_id={"seq": self.peer}, device_id_type=MESH,
                )

            def y(self, side, order, c):
                i = self.base + order * NSC + c
                spot = self.at(side, c)
                return pltpu.make_async_remote_copy(
                    src_ref=self.out.at[spot], dst_ref=self.box.at[spot],
                    send_sem=cs.at[1, i], recv_sem=cr.at[1, i],
                    device_id={"seq": partner}, device_id_type=MESH,
                )

            def serve(self, side, order):
                @pl.loop(0, NSC)
                def _(c):
                    spot = self.at(side, c)
                    z = self.z(side, order, c)

                    @pl.when(jnp.logical_not(self.first))
                    def _():
                        z.wait_recv()

                    had = self.before[spot, :].astype(F32)
                    own = self.own[spot, :].astype(F32)
                    self.ahead[spot, :] = (had + own).astype(BF)

                    @pl.when(jnp.logical_not(self.last))
                    def _():
                        z.start()

                    self.out[spot, :] = (had + self.give * own).astype(BF)
                    self.y(side, order, c).start()

            def finish(self, side, order):
                @pl.loop(0, NSC)
                def _(c):
                    spot = self.at(side, c)
                    self.y(side, order, c).wait()

                    @pl.when(jnp.logical_not(self.last))
                    def _():
                        self.z(side, order, c).wait_send()

                    total = self.before[spot, :].astype(F32) + self.box[spot, :].astype(F32)
                    self.dst[spot, :] = total.astype(BF)

        fwd = Scan(st, sb, pf, nf, of, yf, 0, True)
        bwd = Scan(rv, sa, pb_, nb_, ob, yb, 2 * NSC, False)

        def states(pb):
            for i in range(per):
                ls = lanes(pb, i)
                st[ls, :] = dot(k[:, ls] * live_h, v[:, ls], 0, 0).astype(BF)

        def scores(pb):
            for i in range(per):
                ls = lanes(pb, i)
                s = dot(q[:, ls], k[:, ls], 1, 1) * allowed[...]
                sc[pb * per + i] = s.astype(BF)

        def attend(pb, r):
            for i in range(r * gcols // HD, (r + 1) * gcols // HD):
                ls = lanes(pb, i)
                inner = dot(sc[pb * per + i], v[:, ls], 1, 0) + dot(q[:, ls], sb[ls, :], 1, 0)
                att[:, ls] = (scale * inner).astype(BF)

        def grad_block(pb):
            ga = dot(w_all[wrow(pb), :], go_t[...], 1, 0).astype(BF).T
            g[:, wrow(pb)] = (scale * ga.astype(F32)).astype(BF)
            for i in range(per):
                ls = lanes(pb, i)
                rv[ls, :] = dot(q[:, ls], g[:, ls], 0, 0).astype(BF)

        def grads_within(pb):
            for i in range(per):
                ls = lanes(pb, i)
                gh = g[:, ls]
                inner = (dot(gh, v[:, ls], 1, 1) * allowed[...]).astype(BF)
                gi[pb * per + i] = inner
                dk0[:, ls] = dot(inner, q[:, ls], 0, 0)
                dv0[:, ls] = dot(sc[pb * per + i], gh, 0, 0)

        def grads_query(pb):
            for i in range(per):
                ls = lanes(pb, i)
                inner = gi[pb * per + i]
                dq[:, ls] = (dot(inner, k[:, ls], 1, 0) + dot(g[:, ls], sb[ls, :], 1, 1)).astype(BF)

        def finals(pb):
            for i in range(per):
                ls = lanes(pb, i)
                dk[:, ls] = (dk0[:, ls] + live * dot(v[:, ls], sa[ls, :], 1, 1)).astype(BF)
                dv[:, ls] = (dv0[:, ls] + live * dot(k[:, ls], sa[ls, :], 1, 0)).astype(BF)

        low = zi < m // 2
        high = zi >= m // 2

        loads[0].wait()
        loads[1].wait()
        each_block(far, states)

        @pl.when(fwd.first)
        def _():
            fwd.serve(far, 0)

        each_block(near, states)

        @pl.when(fwd.first)
        def _():
            fwd.serve(near, 1)

        loads[2].wait()
        loads[3].wait()

        @pl.loop(0, width // gcols)
        def _(j):
            cols = pl.ds(pl.multiple_of(j * gcols, gcols), gcols)
            go_t[cols, :] = go_all[grow(me), cols].T

        loads[4].wait()
        grad_block(me)
        w_sib.wait()
        grad_block(sib)

        @pl.when(bwd.first)
        def _():
            bwd.serve(near, 0)

        row_i = lax.broadcasted_iota(jnp.int32, (rows, rows), 0)
        col_i = lax.broadcasted_iota(jnp.int32, (rows, rows), 1)
        rb, cb = row_i // (rows // nb), col_i // (rows // nb)
        keep = jnp.where(rb == cb, 1.0, 0.0).astype(F32)
        for i in range(nb):
            for j in range(i):
                on = jnp.where(vm[0, 0, i, j] == 1, 1.0, 0.0).astype(F32)
                keep = keep + jnp.where((rb == i) & (cb == j), on, 0.0)
        allowed[...] = jnp.where(row_i >= col_i, keep, 0.0) * live * live_r

        each_block(far, scores)

        @pl.when(low & jnp.logical_not(fwd.first))
        def _():
            fwd.serve(far, 0)
            fwd.serve(near, 1)

        each_block(near, scores)

        @pl.when(high & jnp.logical_not(fwd.last))
        def _():
            fwd.serve(far, 0)
            fwd.serve(near, 1)

        each_block(near, grads_within)

        @pl.when(fwd.last)
        def _():
            fwd.serve(far, 0)

        w_x[0].wait()
        w_x[1].wait()

        @pl.when(low)
        def _():
            w_z[0].start()
            w_y[0].start()
            w_z[1].start()

        fwd.finish(far, 0)
        for r, out in enumerate(att_out):
            each_block(far, lambda pb: attend(pb, r))
            out[0].start()
            out[1].start()
        for copy in g_x[1]:
            copy.start()

        @pl.when(fwd.last)
        def _():
            fwd.serve(near, 1)

        @pl.when(high)
        def _():
            w_z[0].start()
            w_y[0].start()
            w_z[1].start()

        relay["x"][0].start()
        relay["x"][1].start()
        w_x[2].wait()
        w_z[2].start()
        relay["x"][2].start()

        fwd.finish(near, 1)
        for r, out in enumerate(att_out):
            each_block(near, lambda pb: attend(pb, r))
            out[2].start()
        each_block(near, grads_query)

        @pl.when(high & jnp.logical_not(bwd.first))
        def _():
            bwd.serve(near, 0)

        w_z[0].wait()
        w_y[1].start()
        relay["z"][0].start()
        go_sib.wait()
        wait(g_x[0])
        for copy in g_relay[0]:
            copy.start()

        def product(r, cols):
            return dot(att_t[span(r), :], go_all[:, cols], 1, 0)

        def cols_of(i):
            return pl.ds(pl.multiple_of(i * piece, HD), piece)

        def second_half():
            wait(g_x[1])
            for copy in g_relay[1]:
                copy.start()
            wait(g_relay[1])

        def turned(r):
            att_t[span(r), grow(me)] = att[:, acol(me, r)].T
            for peer, copy in zip((sib, xp, diag), (att_out[r][2], att_out[r][0], att_out[r][1])):
                copy.wait()
                att_t[span(r), grow(peer)] = attc[peer, :, spans[r]].T

        def hop(i):
            return (zi + (i + m // 2 - 1) % (m - 1) + 1 + (i // (m - 1)) * (m // 2)) % m

        def to_y(r, i):
            to = hop(i)
            at = n_y[0] + r * m + i
            return pltpu.make_async_remote_copy(
                src_ref=part.at[to * 2 + yo, span(r)], dst_ref=pbox.at[to, span(r)],
                send_sem=ys.at[at], recv_sem=yr.at[at],
                device_id={"seq": partner}, device_id_type=MESH,
            )

        def to_z(r, i):
            to = hop(i)
            at = n_z[0] + r * m + i
            return pltpu.make_async_remote_copy(
                src_ref=part.at[to * 2 + yi, span(r)], dst_ref=zpart.at[i, span(r)],
                send_sem=zs.at[at], recv_sem=zr.at[at],
                device_id={"seq": to * 2 + yi}, device_id_type=MESH,
            )

        def begin(r):
            turned(r)
            if piece == gcols:
                @pl.loop(0, m)
                def _(i):
                    spot = hop(i) * 2 + yo
                    part[spot, span(r), :] = product(r, cols_of(spot)).astype(BF)
                    to_y(r, i).start()

        wait(g_relay[0])
        begin(0)

        @pl.when(low & jnp.logical_not(bwd.last))
        def _():
            bwd.serve(near, 0)

        w_y[0].wait()
        relay["y"][0].start()
        w_z[1].wait()
        relay["z"][1].start()
        w_z[2].wait()
        relay["z"][2].start()
        w_y[1].wait()
        relay["y"][1].start()
        grad_block(xp)
        for name in ("x", "z", "y"):
            wait(relay[name])
        grad_block(diag)

        @pl.when(bwd.first)
        def _():
            bwd.serve(far, 1)

        @pl.when(bwd.last)
        def _():
            bwd.serve(near, 0)

        for r in range(1, turns):
            begin(r)

        if piece != gcols:
            second_half()
            for r in range(turns):
                for j in range(width // 256):
                    acc = product(r, slice(j * 256, (j + 1) * 256))
                    for i in range(256 // piece):
                        spot = acc[:, i * piece : (i + 1) * piece]
                        part[j * (256 // piece) + i, spans[r], :] = spot.astype(BF)

                @pl.loop(0, m)
                def _(i):
                    to_y(r, i).start()

        each_block(far, grads_within)

        @pl.when(high & jnp.logical_not(bwd.first))
        def _():
            bwd.serve(far, 1)

        @pl.loop(0, width // 256)
        def _(j):
            cols = pl.ds(pl.multiple_of(j * 256, 256), 256)
            mixed[:, cols] = dot(att[...], w_all[:, cols], 1, 0).astype(BF)

        if piece == gcols:
            second_half()

        def settle(r):
            @pl.loop(0, m)
            def _(i):
                to = hop(i)
                mine = to * 2 + yi
                if piece == gcols:
                    acc = product(r, cols_of(mine))
                else:
                    acc = part[mine, span(r), :].astype(F32)
                to_y(r, i).wait()
                acc = acc + pbox[to, span(r), :].astype(F32)
                part[mine, span(r), :] = acc.astype(BF)

                @pl.when(i < m - 1)
                def _():
                    to_z(r, i).start()

        settle(0)

        @pl.when(low & jnp.logical_not(bwd.last))
        def _():
            bwd.serve(far, 1)

        each_block(far, grads_query)
        bwd.finish(near, 0)
        each_block(near, finals)

        for r in range(1, turns):
            settle(r)
        @pl.when(bwd.last)
        def _():
            bwd.serve(far, 1)

        bwd.finish(far, 1)
        each_block(far, finals)

        total = part[zi * 2 + yi].astype(F32)
        for i in range(m - 1):
            for r in range(turns):
                to_z(r, i).wait()
            total = total + zpart[i].astype(F32)
        wg[...] = total * grad_scale

    vmem = pltpu.VMEM
    sems = pltpu.SemaphoreType.DMA
    state = vmem((heads * HD, HD), BF)
    n_pat = 2 + 3 + NW + 4 * gcount + 3 * turns
    n_y = 2 + m * turns
    n_z = 3 + m * turns
    line = vmem((rows, width), BF)
    scratch = [
        line, line, line,
        vmem((width, rows), BF),
        vmem((width, width), BF),
        vmem((np_ * rows, width), BF),
        line,
        vmem((np_, rows, blk), BF),
        vmem((blk, np_ * rows), BF),
        vmem((heads, rows, rows), BF),
        vmem((heads, rows, rows), BF),
        vmem((rows, rows), F32),
        vmem((rows, width), BF),
        vmem((rows, width), F32),
        vmem((rows, width), F32),
        *[state] * 4,
        *[state] * 8,
        vmem((n, blk, piece), BF),
        vmem((m, blk, piece), BF),
        vmem((m, blk, piece), BF),
        sems((5,)),
        sems((n_pat,)), sems((n_pat,)),
        sems((n_y,)), sems((n_y,)),
        sems((n_z,)), sems((n_z,)),
        sems((2, 4 * NSC)), sems((2, 4 * NSC)),
    ]
    full = pltpu.VMEM((rows, width), BF)
    whole = pl.BlockSpec(memory_space=pltpu.VMEM)
    outside = pl.BlockSpec(memory_space=pltpu.HBM)
    grant = 54
    scalar = pl.BlockSpec(memory_space=pltpu.SMEM)
    return pl.pallas_call(
        kernel,
        out_shape=(full, full, full, full, pltpu.VMEM((blk, piece), F32)),
        in_specs=[outside] * 5 + [scalar] * 2,
        out_specs=(whole,) * 5,
        scratch_shapes=scratch,
        compiler_params=pltpu.CompilerParams(
            collective_id=0, has_side_effects=True, vmem_limit_bytes=grant * 1024 * 1024
        ),
    )


def hand_over(arrays):
    cuts = 2

    def kernel(*refs):
        n = len(arrays)
        src, dst, sem = refs[:n], refs[n : 2 * n], refs[2 * n]
        copies = []
        for i, a in enumerate(arrays):
            r = a.shape[0] // cuts
            for c in range(cuts):
                at = pl.ds(c * r, r)
                copies.append(pltpu.make_async_copy(src[i].at[at], dst[i].at[at], sem.at[i, c]))
        for copy in copies:
            copy.start()
        for copy in copies:
            copy.wait()

    anywhere = pl.BlockSpec(memory_space=pl.ANY)
    return pl.pallas_call(
        kernel,
        out_shape=tuple(jax.ShapeDtypeStruct(a.shape, a.dtype) for a in arrays),
        in_specs=[anywhere] * len(arrays),
        out_specs=(anywhere,) * len(arrays),
        scratch_shapes=[pltpu.SemaphoreType.DMA((len(arrays), cuts))],
        compiler_params=pltpu.CompilerParams(vmem_limit_bytes=1024 * 1024),
    )(*[pltpu.with_memory_space_constraint(a, pltpu.VMEM) for a in arrays])


def solution(mesh):
    n, np_ = mesh.shape["seq"], mesh.shape["pat"]

    def on_device(queries, key_rows, value_rows, out_weight, grad_out, visit_mask, lengths):
        rows, width = queries.shape[1:]
        call = make_kernel(
            n, np_, rows, width, visit_mask.shape[-1], 1.0 / math.sqrt(np_ * n * rows)
        )
        big = [queries[0], key_rows[0], value_rows[0], grad_out[0], out_weight]
        big = [pltpu.with_memory_space_constraint(a, pltpu.HBM) for a in big]
        mixed, dq, dk, dv, wg = call(*big, visit_mask, lengths)
        mixed, dq, dk, dv, wg = hand_over((mixed, dq, dk, dv, wg))
        return mixed[None], dq[None], dk[None], dv[None], wg

    rows3 = P("pat", "seq", None)
    return jax.shard_map(
        on_device,
        mesh=mesh,
        in_specs=(rows3, rows3, rows3, P("pat", None), rows3, P("pat", "seq", None, None), P("pat")),
        out_specs=(rows3, rows3, rows3, rows3, P("pat", "seq")),
        check_vma=False,
    )
```

```python
import math

import jax
import jax.numpy as jnp
from jax import lax
from jax.experimental import pallas as pl
from jax.experimental.pallas import tpu as pltpu
from jax.sharding import PartitionSpec as P

HD = 128
NW = 8
NSC = 4
MESH = pl.DeviceIdType.MESH
F32 = jnp.float32
BF = jnp.bfloat16


def dot(a, b, ca, cb):
    return lax.dot_general(a, b, (((ca,), (cb,)), ((), ())), preferred_element_type=F32)


def make_kernel(n, np_, rows, width, nb, grad_scale):
    heads = width // HD
    per = heads // np_
    blk = per * HD
    piece = width // n
    m = n // 2
    pairs = np_ // 2
    half_rows = heads * HD // 2
    crows = half_rows // NSC
    wrows = blk // NW
    gcols = 256
    gcount = width // (2 * gcols)
    turns = blk // gcols

    def kernel(
        q_hbm, k_hbm, v_hbm, go, w, vm, ln,
        mixed, dq, dk, dv, wg,
        q, k, v, w_all, go_all, att, attc, att_t, sc, gi, allowed, g, dk0, dv0,
        st, sb, rv, sa,
        pf, nf, of, yf, pb_, nb_, ob, yb,
        part, pbox, zpart,
        lsem, ps, pr, ys, yr, zs, zr, cs, cr,
    ):
        me = lax.axis_index("pat")
        si = lax.axis_index("seq")
        sib = me + 1 - 2 * (me % 2)
        xp = (me + 2) % np_
        diag = (sib + 2) % np_
        cx = me // 2
        yi = si % 2
        zi = si // 2
        yo = 1 - yi
        zb = zi % 2
        partner = si + 1 - 2 * yi

        def zpeer(d):
            return ((zi + d) % m) * 2 + yi

        def wrow(p):
            return pl.ds(pl.multiple_of(p * blk, blk), blk)

        def grow(p):
            return pl.ds(pl.multiple_of(p * rows, rows), rows)

        loads = [
            pltpu.make_async_copy(a, b, lsem.at[i])
            for i, (a, b) in enumerate(
                ((k_hbm, k), (v_hbm, v), (q_hbm, q), (go, go_all.at[grow(me)]), (w, w_all.at[wrow(me)]))
            )
        ]
        for copy in loads:
            copy.start()
        barrier = pltpu.get_barrier_semaphore()
        for peer in (sib, xp, diag):
            pl.semaphore_signal(barrier, inc=1, device_id={"pat": peer}, device_id_type=MESH)
        for peer in [partner] + [zpeer(d) for d in range(1, m)]:
            pl.semaphore_signal(barrier, inc=1, device_id={"seq": peer}, device_id_type=MESH)
        pl.semaphore_wait(barrier, 3 + m)

        n_pat = [0]
        n_y = [0]
        n_z = [0]

        def pat_copy(src, dst, peer):
            i = n_pat[0]
            n_pat[0] += 1
            return pltpu.make_async_remote_copy(
                src_ref=src, dst_ref=dst, send_sem=ps.at[i], recv_sem=pr.at[i],
                device_id={"pat": peer}, device_id_type=MESH,
            )

        def y_copy(src, dst):
            i = n_y[0]
            n_y[0] += 1
            return pltpu.make_async_remote_copy(
                src_ref=src, dst_ref=dst, send_sem=ys.at[i], recv_sem=yr.at[i],
                device_id={"seq": partner}, device_id_type=MESH,
            )

        def z_copy(src, dst, peer):
            i = n_z[0]
            n_z[0] += 1
            return pltpu.make_async_remote_copy(
                src_ref=src, dst_ref=dst, send_sem=zs.at[i], recv_sem=zr.at[i],
                device_id={"seq": peer}, device_id_type=MESH,
            )

        def wsl(c, p=0):
            return pl.ds(pl.multiple_of(p * blk + c * wrows, wrows), wrows)

        w_sib = pat_copy(w, w_all.at[wrow(me)], sib)
        go_sib = pat_copy(go, go_all.at[grow(me)], sib)

        zpair = (zi + 1 - 2 * zb) * 2 + yi
        x_set = [4 + 2 * yi + zb, 2 * zb, 2 * zb + 1]
        z_set = [5 + 2 * yi - zb, 2 - 2 * zb, 3 - 2 * zb]
        y_set = [4 + 2 * yo + zb, 5 + 2 * yo - zb]

        def far_w(c):
            return w_all.at[wsl(c, xp)]

        w_x = [pat_copy(w.at[wsl(c)], w_all.at[wsl(c, me)], xp) for c in x_set]
        w_z = [z_copy(far_w(c), far_w(c), zpair) for c in x_set]
        w_y = [y_copy(far_w(c), far_w(c)) for c in (x_set[0], z_set[0])]
        relay = {}
        for name, group in (("x", x_set), ("z", z_set), ("y", y_set)):
            relay[name] = [pat_copy(far_w(c), far_w(c), sib) for c in group]

        def gsl(t, odd):
            return pl.ds(pl.multiple_of((2 * t + odd) * gcols, gcols), gcols)

        g_x, g_relay = [], []
        for odd in (yo, yi):
            cols = [gsl(t, odd) for t in range(gcount)]
            g_x.append([pat_copy(go.at[:, c], go_all.at[grow(me), c], xp) for c in cols])
            g_relay.append([pat_copy(go_all.at[grow(xp), c], go_all.at[grow(xp), c], sib) for c in cols])
        spans = [slice(r * gcols, (r + 1) * gcols) for r in range(turns)]

        def span(r):
            return pl.ds(r * gcols, gcols)

        def acol(p, r):
            return pl.ds(pl.multiple_of(p * blk + r * gcols, gcols), gcols)

        att_out = [
            [pat_copy(att.at[:, acol(p, r)], attc.at[me, :, spans[r]], p) for p in (xp, diag, sib)]
            for r in range(turns)
        ]

        for copy in w_x:
            copy.start()
        w_sib.start()
        go_sib.start()
        for copy in g_x[0]:
            copy.start()

        pos_c = si * rows + lax.broadcasted_iota(jnp.int32, (rows, 1), 0)
        pos_r = si * rows + lax.broadcasted_iota(jnp.int32, (1, rows), 1)
        live = jnp.where(pos_c < ln[0], 1.0, 0.0).astype(F32)
        live_r = jnp.where(pos_r < ln[0], 1.0, 0.0).astype(F32)
        live_h = live.astype(BF)
        scale = live * lax.rsqrt((pos_c + 1).astype(F32)) / math.sqrt(HD)

        def wait(copies):
            for copy in copies:
                copy.wait()

        def lanes(pb, i, size=HD):
            return pl.ds(pl.multiple_of(pb * blk + i * HD, HD), size)

        near, far = cx, 1 - cx

        def each_block(side, body):
            @pl.loop(0, pairs)
            def _(t):
                body(side * pairs + t)

        class Scan:
            def __init__(self, own, dst, before, ahead, out, box, base, forward):
                self.own, self.dst, self.before, self.ahead = own, dst, before, ahead
                self.out, self.box, self.base, self.forward = out, box, base, forward
                step = 1 if forward else m - 1
                self.peer = zpeer(step)
                self.first = zi == (0 if forward else m - 1)
                self.last = zi == (m - 1 if forward else 0)
                self.give = (yo if forward else yi).astype(F32)

                @pl.when(self.first)
                def _():
                    self.before[...] = jnp.zeros_like(self.before)

            def at(self, side, c):
                return pl.ds(pl.multiple_of(side * half_rows + c * crows, crows), crows)

            def z(self, side, order, c):
                i = self.base + order * NSC + c
                spot = self.at(side, c)
                return pltpu.make_async_remote_copy(
                    src_ref=self.ahead.at[spot], dst_ref=self.before.at[spot],
                    send_sem=cs.at[0, i], recv_sem=cr.at[0, i],
                    device_id={"seq": self.peer}, device_id_type=MESH,
                )

            def y(self, side, order, c):
                i = self.base + order * NSC + c
                spot = self.at(side, c)
                return pltpu.make_async_remote_copy(
                    src_ref=self.out.at[spot], dst_ref=self.box.at[spot],
                    send_sem=cs.at[1, i], recv_sem=cr.at[1, i],
                    device_id={"seq": partner}, device_id_type=MESH,
                )

            def serve(self, side, order, pass_on=True):
                @pl.loop(0, NSC)
                def _(c):
                    spot = self.at(side, c)
                    z = self.z(side, order, c)

                    @pl.when(jnp.logical_not(self.first))
                    def _():
                        z.wait_recv()

                    had = self.before[spot, :].astype(F32)
                    own = self.own[spot, :].astype(F32)
                    self.ahead[spot, :] = (had + own).astype(BF)

                    @pl.when(jnp.logical_not(self.last))
                    def _():
                        z.start()

                    self.out[spot, :] = (had + self.give * own).astype(BF)
                    if pass_on:
                        self.y(side, order, c).start()

            def send(self, side, order):
                @pl.loop(0, NSC)
                def _(c):
                    self.y(side, order, c).start()

            def finish(self, side, order):
                @pl.loop(0, NSC)
                def _(c):
                    spot = self.at(side, c)
                    self.y(side, order, c).wait()

                    @pl.when(jnp.logical_not(self.last))
                    def _():
                        self.z(side, order, c).wait_send()

                    total = self.before[spot, :].astype(F32) + self.box[spot, :].astype(F32)
                    self.dst[spot, :] = total.astype(BF)

        fwd = Scan(st, sb, pf, nf, of, yf, 0, True)
        bwd = Scan(rv, sa, pb_, nb_, ob, yb, 2 * NSC, False)

        def states(pb):
            for i in range(per):
                ls = lanes(pb, i)
                st[ls, :] = dot(k[:, ls] * live_h, v[:, ls], 0, 0).astype(BF)

        def scores(pb):
            for i in range(per):
                ls = lanes(pb, i)
                s = dot(q[:, ls], k[:, ls], 1, 1) * allowed[...]
                sc[pb * per + i] = s.astype(BF)

        def attend(pb, r):
            for i in range(r * gcols // HD, (r + 1) * gcols // HD):
                ls = lanes(pb, i)
                inner = dot(sc[pb * per + i], v[:, ls], 1, 0) + dot(q[:, ls], sb[ls, :], 1, 0)
                att[:, ls] = (scale * inner).astype(BF)

        def grad_block(pb):
            ga = dot(go_all[grow(me), :], w_all[wrow(pb), :], 1, 1).astype(BF)
            gg = (scale * ga.astype(F32)).astype(BF)
            g[:, wrow(pb)] = gg
            for i in range(per):
                ls = lanes(pb, i)
                rv[ls, :] = dot(q[:, ls], gg[:, i * HD : (i + 1) * HD], 0, 0).astype(BF)

        def grads_within(pb):
            for i in range(per):
                ls = lanes(pb, i)
                gh = g[:, ls]
                inner = (dot(gh, v[:, ls], 1, 1) * allowed[...]).astype(BF)
                gi[pb * per + i] = inner
                dk0[:, ls] = dot(inner, q[:, ls], 0, 0)
                dv0[:, ls] = dot(sc[pb * per + i], gh, 0, 0)

        def grads_query(pb):
            for i in range(per):
                ls = lanes(pb, i)
                inner = gi[pb * per + i]
                dq[:, ls] = (dot(inner, k[:, ls], 1, 0) + dot(g[:, ls], sb[ls, :], 1, 1)).astype(BF)

        def finals(pb):
            for i in range(per):
                ls = lanes(pb, i)
                dk[:, ls] = (dk0[:, ls] + live * dot(v[:, ls], sa[ls, :], 1, 1)).astype(BF)
                dv[:, ls] = (dv0[:, ls] + live * dot(k[:, ls], sa[ls, :], 1, 0)).astype(BF)

        low = zi < m // 2
        high = zi >= m // 2

        loads[0].wait()
        loads[1].wait()
        each_block(far, states)

        @pl.when(fwd.first)
        def _():
            fwd.serve(far, 0)

        each_block(near, states)

        @pl.when(fwd.first)
        def _():
            fwd.serve(near, 1)

        loads[2].wait()
        loads[3].wait()

        loads[4].wait()
        grad_block(me)
        w_sib.wait()
        grad_block(sib)

        @pl.when(bwd.first)
        def _():
            bwd.serve(near, 0)

        row_i = lax.broadcasted_iota(jnp.int32, (rows, rows), 0)
        col_i = lax.broadcasted_iota(jnp.int32, (rows, rows), 1)
        rb, cb = row_i // (rows // nb), col_i // (rows // nb)
        keep = jnp.where(rb == cb, 1.0, 0.0).astype(F32)
        for i in range(nb):
            for j in range(i):
                on = jnp.where(vm[0, 0, i, j] == 1, 1.0, 0.0).astype(F32)
                keep = keep + jnp.where((rb == i) & (cb == j), on, 0.0)
        allowed[...] = jnp.where(row_i >= col_i, keep, 0.0) * live * live_r

        each_block(far, scores)

        @pl.when(low & jnp.logical_not(fwd.first))
        def _():
            fwd.serve(far, 0)
            fwd.serve(near, 1)

        each_block(near, scores)

        @pl.when(high & jnp.logical_not(fwd.last))
        def _():
            fwd.serve(far, 0)
            fwd.serve(near, 1)

        each_block(near, grads_within)

        w_x[0].wait()
        w_z[0].start()
        w_y[0].start()
        w_x[1].wait()
        w_z[1].start()

        @pl.when(fwd.last)
        def _():
            fwd.serve(far, 0)

        fwd.finish(far, 0)
        for r, out in enumerate(att_out):
            each_block(far, lambda pb: attend(pb, r))
            out[0].start()
            out[1].start()
        for copy in g_x[1]:
            copy.start()

        @pl.when(fwd.last)
        def _():
            fwd.serve(near, 1)

        relay["x"][0].start()
        relay["x"][1].start()
        w_x[2].wait()
        w_z[2].start()
        relay["x"][2].start()

        fwd.finish(near, 1)
        for r, out in enumerate(att_out):
            each_block(near, lambda pb: attend(pb, r))
            out[2].start()
        each_block(near, grads_query)

        @pl.when(high & jnp.logical_not(bwd.first))
        def _():
            bwd.serve(near, 0, False)

        w_z[0].wait()
        w_y[1].start()
        relay["z"][0].start()
        go_sib.wait()
        wait(g_x[0])
        for copy in g_relay[0]:
            copy.start()

        def product(r, cols):
            return dot(att_t[span(r), :], go_all[:, cols], 1, 0)

        def cols_of(i):
            return pl.ds(pl.multiple_of(i * piece, HD), piece)

        def second_half():
            wait(g_x[1])
            for copy in g_relay[1]:
                copy.start()
            wait(g_relay[1])

        def turned(r):
            att_t[span(r), grow(me)] = att[:, acol(me, r)].T
            for peer, copy in zip((sib, xp, diag), (att_out[r][2], att_out[r][0], att_out[r][1])):
                copy.wait()
                att_t[span(r), grow(peer)] = attc[peer, :, spans[r]].T

        def hop(i):
            return (zi + (i + m // 2 - 1) % (m - 1) + 1 + (i // (m - 1)) * (m // 2)) % m

        def to_y(r, i):
            to = hop(i)
            at = n_y[0] + r * m + i
            return pltpu.make_async_remote_copy(
                src_ref=part.at[to * 2 + yo, span(r)], dst_ref=pbox.at[to, span(r)],
                send_sem=ys.at[at], recv_sem=yr.at[at],
                device_id={"seq": partner}, device_id_type=MESH,
            )

        def to_z(r, i):
            to = hop(i)
            at = n_z[0] + r * m + i
            return pltpu.make_async_remote_copy(
                src_ref=part.at[to * 2 + yi, span(r)], dst_ref=zpart.at[i, span(r)],
                send_sem=zs.at[at], recv_sem=zr.at[at],
                device_id={"seq": to * 2 + yi}, device_id_type=MESH,
            )

        def begin(r):
            turned(r)
            if piece == gcols:
                @pl.loop(0, m)
                def _(i):
                    spot = hop(i) * 2 + yo
                    part[spot, span(r), :] = product(r, cols_of(spot)).astype(BF)
                    to_y(r, i).start()

        wait(g_relay[0])
        begin(0)

        @pl.when(low & jnp.logical_not(bwd.last))
        def _():
            bwd.serve(near, 0, False)

        w_y[0].wait()
        relay["y"][0].start()
        w_z[1].wait()
        relay["z"][1].start()
        w_z[2].wait()
        relay["z"][2].start()
        w_y[1].wait()
        relay["y"][1].start()
        grad_block(xp)
        for name in ("x", "z", "y"):
            wait(relay[name])
        grad_block(diag)

        @pl.when(bwd.first)
        def _():
            bwd.serve(far, 1, False)

        @pl.when(bwd.last)
        def _():
            bwd.serve(near, 0, False)

        for r in range(1, turns):
            begin(r)

        @pl.when(jnp.logical_not(bwd.first))
        def _():
            bwd.send(near, 0)

        @pl.when(bwd.first)
        def _():
            bwd.send(far, 1)

        if piece != gcols:
            second_half()
            for r in range(turns):
                for j in range(width // 256):
                    acc = product(r, slice(j * 256, (j + 1) * 256))
                    for i in range(256 // piece):
                        spot = acc[:, i * piece : (i + 1) * piece]
                        part[j * (256 // piece) + i, spans[r], :] = spot.astype(BF)

                @pl.loop(0, m)
                def _(i):
                    to_y(r, i).start()

        each_block(far, grads_within)

        @pl.when(high & jnp.logical_not(bwd.first))
        def _():
            bwd.serve(far, 1)

        wide = width // 2

        @pl.loop(0, 2)
        def _(j):
            cols = pl.ds(pl.multiple_of(j * wide, wide), wide)
            mixed[:, cols] = dot(att[...], w_all[:, cols], 1, 0).astype(BF)

        @pl.when(low & jnp.logical_not(bwd.last))
        def _():
            bwd.serve(far, 1)

        if piece == gcols:
            second_half()

        def settle(r):
            @pl.loop(0, m)
            def _(i):
                to = hop(i)
                mine = to * 2 + yi
                if piece == gcols:
                    acc = product(r, cols_of(mine))
                else:
                    acc = part[mine, span(r), :].astype(F32)
                to_y(r, i).wait()
                acc = acc + pbox[to, span(r), :].astype(F32)
                part[mine, span(r), :] = acc.astype(BF)

                @pl.when(i < m - 1)
                def _():
                    to_z(r, i).start()

        settle(0)

        each_block(far, grads_query)

        for r in range(1, turns):
            settle(r)
        @pl.when(bwd.last)
        def _():
            bwd.serve(far, 1)

        bwd.finish(near, 0)
        each_block(near, finals)
        bwd.finish(far, 1)
        each_block(far, finals)

        total = part[zi * 2 + yi].astype(F32)
        for i in range(m - 1):
            for r in range(turns):
                to_z(r, i).wait()
            total = total + zpart[i].astype(F32)
        wg[...] = total * grad_scale

    vmem = pltpu.VMEM
    sems = pltpu.SemaphoreType.DMA
    state = vmem((heads * HD, HD), BF)
    n_pat = 2 + 3 + NW + 4 * gcount + 3 * turns
    n_y = 2 + m * turns
    n_z = 3 + m * turns
    line = vmem((rows, width), BF)
    scratch = [
        line, line, line,
        vmem((width, width), BF),
        vmem((np_ * rows, width), BF),
        line,
        vmem((np_, rows, blk), BF),
        vmem((blk, np_ * rows), BF),
        vmem((heads, rows, rows), BF),
        vmem((heads, rows, rows), BF),
        vmem((rows, rows), F32),
        vmem((rows, width), BF),
        vmem((rows, width), F32),
        vmem((rows, width), F32),
        *[state] * 4,
        *[state] * 8,
        vmem((n, blk, piece), BF),
        vmem((m, blk, piece), BF),
        vmem((m, blk, piece), BF),
        sems((5,)),
        sems((n_pat,)), sems((n_pat,)),
        sems((n_y,)), sems((n_y,)),
        sems((n_z,)), sems((n_z,)),
        sems((2, 4 * NSC)), sems((2, 4 * NSC)),
    ]
    full = pltpu.VMEM((rows, width), BF)
    whole = pl.BlockSpec(memory_space=pltpu.VMEM)
    outside = pl.BlockSpec(memory_space=pltpu.HBM)
    grant = 54
    scalar = pl.BlockSpec(memory_space=pltpu.SMEM)
    return pl.pallas_call(
        kernel,
        out_shape=(full, full, full, full, pltpu.VMEM((blk, piece), F32)),
        in_specs=[outside] * 5 + [scalar] * 2,
        out_specs=(whole,) * 5,
        scratch_shapes=scratch,
        compiler_params=pltpu.CompilerParams(
            collective_id=0, has_side_effects=True, vmem_limit_bytes=grant * 1024 * 1024
        ),
    )


def hand_over(arrays):
    cuts = 2

    def kernel(*refs):
        n = len(arrays)
        src, dst, sem = refs[:n], refs[n : 2 * n], refs[2 * n]
        copies = []
        for i, a in enumerate(arrays):
            r = a.shape[0] // cuts
            for c in range(cuts):
                at = pl.ds(c * r, r)
                copies.append(pltpu.make_async_copy(src[i].at[at], dst[i].at[at], sem.at[i, c]))
        for copy in copies:
            copy.start()
        for copy in copies:
            copy.wait()

    anywhere = pl.BlockSpec(memory_space=pl.ANY)
    return pl.pallas_call(
        kernel,
        out_shape=tuple(jax.ShapeDtypeStruct(a.shape, a.dtype) for a in arrays),
        in_specs=[anywhere] * len(arrays),
        out_specs=(anywhere,) * len(arrays),
        scratch_shapes=[pltpu.SemaphoreType.DMA((len(arrays), cuts))],
        compiler_params=pltpu.CompilerParams(vmem_limit_bytes=1024 * 1024),
    )(*[pltpu.with_memory_space_constraint(a, pltpu.VMEM) for a in arrays])


def solution(mesh):
    n, np_ = mesh.shape["seq"], mesh.shape["pat"]

    def on_device(queries, key_rows, value_rows, out_weight, grad_out, visit_mask, lengths):
        rows, width = queries.shape[1:]
        call = make_kernel(
            n, np_, rows, width, visit_mask.shape[-1], 1.0 / math.sqrt(np_ * n * rows)
        )
        big = [queries[0], key_rows[0], value_rows[0], grad_out[0], out_weight]
        big = [pltpu.with_memory_space_constraint(a, pltpu.HBM) for a in big]
        mixed, dq, dk, dv, wg = call(*big, visit_mask, lengths)
        mixed, dq, dk, dv, wg = hand_over((mixed, dq, dk, dv, wg))
        return mixed[None], dq[None], dk[None], dv[None], wg

    rows3 = P("pat", "seq", None)
    return jax.shard_map(
        on_device,
        mesh=mesh,
        in_specs=(rows3, rows3, rows3, P("pat", None), rows3, P("pat", "seq", None, None), P("pat")),
        out_specs=(rows3, rows3, rows3, rows3, P("pat", "seq")),
        check_vma=False,
    )
```

```python
import math

import jax
import jax.numpy as jnp
from jax import lax
from jax.experimental import pallas as pl
from jax.experimental.pallas import tpu as pltpu
from jax.sharding import PartitionSpec as P

HD = 128
NW = 8
NSC = 2
MESH = pl.DeviceIdType.MESH
F32 = jnp.float32
BF = jnp.bfloat16


def dot(a, b, ca, cb):
    return lax.dot_general(a, b, (((ca,), (cb,)), ((), ())), preferred_element_type=F32)


def make_kernel(n, np_, rows, width, nb, grad_scale):
    heads = width // HD
    per = heads // np_
    blk = per * HD
    piece = width // n
    m = n // 2
    pairs = np_ // 2
    half_rows = heads * HD // 2
    crows = half_rows // NSC
    wrows = blk // NW
    gcols = 256
    gcount = width // (2 * gcols)
    turns = blk // gcols

    def kernel(
        q_hbm, k_hbm, v_hbm, go, w, vm, ln,
        mixed, dq, dk, dv, wg,
        q, k, v, w_all, go_all, att, attc, att_t, sc, gi, allowed, g, dk0, dv0,
        st, sb, rv, sa,
        pf, nf, of, yf, pb_, nb_, ob, yb,
        part, pbox, zpart,
        lsem, ps, pr, ys, yr, zs, zr, cs, cr,
    ):
        me = lax.axis_index("pat")
        si = lax.axis_index("seq")
        sib = me + 1 - 2 * (me % 2)
        xp = (me + 2) % np_
        diag = (sib + 2) % np_
        cx = me // 2
        yi = si % 2
        zi = si // 2
        yo = 1 - yi
        zb = zi % 2
        partner = si + 1 - 2 * yi

        def zpeer(d):
            return ((zi + d) % m) * 2 + yi

        def wrow(p):
            return pl.ds(pl.multiple_of(p * blk, blk), blk)

        def grow(p):
            return pl.ds(pl.multiple_of(p * rows, rows), rows)

        loads = [
            pltpu.make_async_copy(a, b, lsem.at[i])
            for i, (a, b) in enumerate(
                ((k_hbm, k), (v_hbm, v), (q_hbm, q), (go, go_all.at[grow(me)]), (w, w_all.at[wrow(me)]))
            )
        ]
        for copy in loads:
            copy.start()
        barrier = pltpu.get_barrier_semaphore()
        for peer in (sib, xp, diag):
            pl.semaphore_signal(barrier, inc=1, device_id={"pat": peer}, device_id_type=MESH)
        for peer in [partner] + [zpeer(d) for d in range(1, m)]:
            pl.semaphore_signal(barrier, inc=1, device_id={"seq": peer}, device_id_type=MESH)
        pl.semaphore_wait(barrier, 3 + m)

        n_pat = [0]
        n_y = [0]
        n_z = [0]

        def pat_copy(src, dst, peer):
            i = n_pat[0]
            n_pat[0] += 1
            return pltpu.make_async_remote_copy(
                src_ref=src, dst_ref=dst, send_sem=ps.at[i], recv_sem=pr.at[i],
                device_id={"pat": peer}, device_id_type=MESH,
            )

        def y_copy(src, dst):
            i = n_y[0]
            n_y[0] += 1
            return pltpu.make_async_remote_copy(
                src_ref=src, dst_ref=dst, send_sem=ys.at[i], recv_sem=yr.at[i],
                device_id={"seq": partner}, device_id_type=MESH,
            )

        def z_copy(src, dst, peer):
            i = n_z[0]
            n_z[0] += 1
            return pltpu.make_async_remote_copy(
                src_ref=src, dst_ref=dst, send_sem=zs.at[i], recv_sem=zr.at[i],
                device_id={"seq": peer}, device_id_type=MESH,
            )

        def wsl(c, p=0):
            return pl.ds(pl.multiple_of(p * blk + c * wrows, wrows), wrows)

        w_sib = pat_copy(w, w_all.at[wrow(me)], sib)
        go_sib = pat_copy(go, go_all.at[grow(me)], sib)

        zpair = (zi + 1 - 2 * zb) * 2 + yi
        x_set = [4 + 2 * yi + zb, 2 * zb, 2 * zb + 1]
        z_set = [5 + 2 * yi - zb, 2 - 2 * zb, 3 - 2 * zb]
        y_set = [4 + 2 * yo + zb, 5 + 2 * yo - zb]

        def far_w(c):
            return w_all.at[wsl(c, xp)]

        w_x = [pat_copy(w.at[wsl(c)], w_all.at[wsl(c, me)], xp) for c in x_set]
        w_z = [z_copy(far_w(c), far_w(c), zpair) for c in x_set]
        w_y = [y_copy(far_w(c), far_w(c)) for c in (x_set[0], z_set[0])]
        relay = {}
        for name, group in (("x", x_set), ("z", z_set), ("y", y_set)):
            relay[name] = [pat_copy(far_w(c), far_w(c), sib) for c in group]

        def gsl(t, odd):
            return pl.ds(pl.multiple_of((2 * t + odd) * gcols, gcols), gcols)

        g_x, g_relay = [], []
        for odd in (yo, yi):
            cols = [gsl(t, odd) for t in range(gcount)]
            g_x.append([pat_copy(go.at[:, c], go_all.at[grow(me), c], xp) for c in cols])
            g_relay.append([pat_copy(go_all.at[grow(xp), c], go_all.at[grow(xp), c], sib) for c in cols])
        spans = [slice(r * gcols, (r + 1) * gcols) for r in range(turns)]

        def span(r):
            return pl.ds(r * gcols, gcols)

        def acol(p, r):
            return pl.ds(pl.multiple_of(p * blk + r * gcols, gcols), gcols)

        att_out = [
            [pat_copy(att.at[:, acol(p, r)], attc.at[me, :, spans[r]], p) for p in (xp, diag, sib)]
            for r in range(turns)
        ]

        for copy in w_x:
            copy.start()
        w_sib.start()
        go_sib.start()
        for copy in g_x[0]:
            copy.start()

        pos_c = si * rows + lax.broadcasted_iota(jnp.int32, (rows, 1), 0)
        pos_r = si * rows + lax.broadcasted_iota(jnp.int32, (1, rows), 1)
        live = jnp.where(pos_c < ln[0], 1.0, 0.0).astype(F32)
        live_r = jnp.where(pos_r < ln[0], 1.0, 0.0).astype(F32)
        live_h = live.astype(BF)
        scale = live * lax.rsqrt((pos_c + 1).astype(F32)) / math.sqrt(HD)

        def wait(copies):
            for copy in copies:
                copy.wait()

        def lanes(pb, i, size=HD):
            return pl.ds(pl.multiple_of(pb * blk + i * HD, HD), size)

        near, far = cx, 1 - cx

        def each_block(side, body):
            @pl.loop(0, pairs)
            def _(t):
                body(side * pairs + t)

        class Scan:
            def __init__(self, own, dst, before, ahead, out, box, base, forward):
                self.own, self.dst, self.before, self.ahead = own, dst, before, ahead
                self.out, self.box, self.base, self.forward = out, box, base, forward
                step = 1 if forward else m - 1
                self.peer = zpeer(step)
                self.first = zi == (0 if forward else m - 1)
                self.last = zi == (m - 1 if forward else 0)
                self.give = (yo if forward else yi).astype(F32)

                @pl.when(self.first)
                def _():
                    self.before[...] = jnp.zeros_like(self.before)

            def at(self, side, c):
                return pl.ds(pl.multiple_of(side * half_rows + c * crows, crows), crows)

            def z(self, side, order, c):
                i = self.base + order * NSC + c
                spot = self.at(side, c)
                return pltpu.make_async_remote_copy(
                    src_ref=self.ahead.at[spot], dst_ref=self.before.at[spot],
                    send_sem=cs.at[0, i], recv_sem=cr.at[0, i],
                    device_id={"seq": self.peer}, device_id_type=MESH,
                )

            def y(self, side, order, c):
                i = self.base + order * NSC + c
                spot = self.at(side, c)
                return pltpu.make_async_remote_copy(
                    src_ref=self.out.at[spot], dst_ref=self.box.at[spot],
                    send_sem=cs.at[1, i], recv_sem=cr.at[1, i],
                    device_id={"seq": partner}, device_id_type=MESH,
                )

            def serve(self, side, order, pass_on=True):
                @pl.loop(0, NSC)
                def _(c):
                    spot = self.at(side, c)
                    z = self.z(side, order, c)

                    @pl.when(jnp.logical_not(self.first))
                    def _():
                        z.wait_recv()

                    had = self.before[spot, :].astype(F32)
                    own = self.own[spot, :].astype(F32)
                    self.ahead[spot, :] = (had + own).astype(BF)

                    @pl.when(jnp.logical_not(self.last))
                    def _():
                        z.start()

                    self.out[spot, :] = (had + self.give * own).astype(BF)
                    if pass_on:
                        self.y(side, order, c).start()

            def send(self, side, order):
                @pl.loop(0, NSC)
                def _(c):
                    self.y(side, order, c).start()

            def finish(self, side, order):
                @pl.loop(0, NSC)
                def _(c):
                    spot = self.at(side, c)
                    self.y(side, order, c).wait()

                    @pl.when(jnp.logical_not(self.last))
                    def _():
                        self.z(side, order, c).wait_send()

                    total = self.before[spot, :].astype(F32) + self.box[spot, :].astype(F32)
                    self.dst[spot, :] = total.astype(BF)

        fwd = Scan(st, sb, pf, nf, of, yf, 0, True)
        bwd = Scan(rv, sa, pb_, nb_, ob, yb, 2 * NSC, False)

        def states(pb):
            for i in range(per):
                ls = lanes(pb, i)
                st[ls, :] = dot(k[:, ls] * live_h, v[:, ls], 0, 0).astype(BF)

        def scores(pb):
            for i in range(per):
                ls = lanes(pb, i)
                s = dot(q[:, ls], k[:, ls], 1, 1) * allowed[...]
                sc[pb * per + i] = s.astype(BF)

        def attend(pb, r):
            for i in range(r * gcols // HD, (r + 1) * gcols // HD):
                ls = lanes(pb, i)
                inner = dot(sc[pb * per + i], v[:, ls], 1, 0) + dot(q[:, ls], sb[ls, :], 1, 0)
                att[:, ls] = (scale * inner).astype(BF)

        def grad_block(pb):
            ga = dot(go_all[grow(me), :], w_all[wrow(pb), :], 1, 1).astype(BF)
            gg = (scale * ga.astype(F32)).astype(BF)
            g[:, wrow(pb)] = gg
            for i in range(per):
                ls = lanes(pb, i)
                rv[ls, :] = dot(q[:, ls], gg[:, i * HD : (i + 1) * HD], 0, 0).astype(BF)

        def grads_within(pb):
            for i in range(per):
                ls = lanes(pb, i)
                gh = g[:, ls]
                inner = (dot(gh, v[:, ls], 1, 1) * allowed[...]).astype(BF)
                gi[pb * per + i] = inner
                dk0[:, ls] = dot(inner, q[:, ls], 0, 0)
                dv0[:, ls] = dot(sc[pb * per + i], gh, 0, 0)

        def grads_query(pb):
            for i in range(per):
                ls = lanes(pb, i)
                inner = gi[pb * per + i]
                dq[:, ls] = (dot(inner, k[:, ls], 1, 0) + dot(g[:, ls], sb[ls, :], 1, 1)).astype(BF)

        def finals(pb):
            for i in range(per):
                ls = lanes(pb, i)
                dk[:, ls] = (dk0[:, ls] + live * dot(v[:, ls], sa[ls, :], 1, 1)).astype(BF)
                dv[:, ls] = (dv0[:, ls] + live * dot(k[:, ls], sa[ls, :], 1, 0)).astype(BF)

        low = zi < m // 2
        high = zi >= m // 2

        loads[0].wait()
        loads[1].wait()
        each_block(far, states)

        @pl.when(fwd.first)
        def _():
            fwd.serve(far, 0)

        each_block(near, states)

        @pl.when(fwd.first)
        def _():
            fwd.serve(near, 1)

        loads[2].wait()
        loads[3].wait()

        loads[4].wait()
        grad_block(me)
        w_sib.wait()
        grad_block(sib)

        @pl.when(bwd.first)
        def _():
            bwd.serve(near, 0)

        row_i = lax.broadcasted_iota(jnp.int32, (rows, rows), 0)
        col_i = lax.broadcasted_iota(jnp.int32, (rows, rows), 1)
        rb, cb = row_i // (rows // nb), col_i // (rows // nb)
        keep = jnp.where(rb == cb, 1.0, 0.0).astype(F32)
        for i in range(nb):
            for j in range(i):
                on = jnp.where(vm[0, 0, i, j] == 1, 1.0, 0.0).astype(F32)
                keep = keep + jnp.where((rb == i) & (cb == j), on, 0.0)
        allowed[...] = jnp.where(row_i >= col_i, keep, 0.0) * live * live_r

        each_block(far, scores)

        @pl.when(low & jnp.logical_not(fwd.first))
        def _():
            fwd.serve(far, 0)
            fwd.serve(near, 1)

        each_block(near, scores)

        @pl.when(high & jnp.logical_not(fwd.last))
        def _():
            fwd.serve(far, 0)
            fwd.serve(near, 1)

        each_block(near, grads_within)

        w_x[0].wait()
        w_z[0].start()
        w_y[0].start()
        w_x[1].wait()
        w_z[1].start()

        @pl.when(fwd.last)
        def _():
            fwd.serve(far, 0)

        fwd.finish(far, 0)
        for r, out in enumerate(att_out):
            each_block(far, lambda pb: attend(pb, r))
            out[0].start()
            out[1].start()
        for copy in g_x[1]:
            copy.start()

        @pl.when(fwd.last)
        def _():
            fwd.serve(near, 1)

        relay["x"][0].start()
        relay["x"][1].start()
        w_x[2].wait()
        w_z[2].start()
        relay["x"][2].start()

        fwd.finish(near, 1)
        for r, out in enumerate(att_out):
            each_block(near, lambda pb: attend(pb, r))
            out[2].start()
        each_block(near, grads_query)

        @pl.when(high & jnp.logical_not(bwd.first))
        def _():
            bwd.serve(near, 0, False)

        w_z[0].wait()
        w_y[1].start()
        relay["z"][0].start()
        go_sib.wait()
        wait(g_x[0])
        for copy in g_relay[0]:
            copy.start()

        def product(r, cols):
            return dot(att_t[span(r), :], go_all[:, cols], 1, 0)

        def cols_of(i):
            return pl.ds(pl.multiple_of(i * piece, HD), piece)

        def second_half():
            wait(g_x[1])
            for copy in g_relay[1]:
                copy.start()
            wait(g_relay[1])

        def turned(r):
            att_t[span(r), grow(me)] = att[:, acol(me, r)].T
            for peer, copy in zip((sib, xp, diag), (att_out[r][2], att_out[r][0], att_out[r][1])):
                copy.wait()
                att_t[span(r), grow(peer)] = attc[peer, :, spans[r]].T

        def hop(i):
            return (zi + (i + m // 2 - 1) % (m - 1) + 1 + (i // (m - 1)) * (m // 2)) % m

        def to_y(r, i):
            to = hop(i)
            at = n_y[0] + r * m + i
            return pltpu.make_async_remote_copy(
                src_ref=part.at[to * 2 + yo, span(r)], dst_ref=pbox.at[to, span(r)],
                send_sem=ys.at[at], recv_sem=yr.at[at],
                device_id={"seq": partner}, device_id_type=MESH,
            )

        def to_z(r, i):
            to = hop(i)
            at = n_z[0] + r * m + i
            return pltpu.make_async_remote_copy(
                src_ref=part.at[to * 2 + yi, span(r)], dst_ref=zpart.at[i, span(r)],
                send_sem=zs.at[at], recv_sem=zr.at[at],
                device_id={"seq": to * 2 + yi}, device_id_type=MESH,
            )

        def begin(r):
            turned(r)
            if piece == gcols:
                @pl.loop(0, m)
                def _(i):
                    spot = hop(i) * 2 + yo
                    part[spot, span(r), :] = product(r, cols_of(spot)).astype(BF)
                    to_y(r, i).start()

        wait(g_relay[0])
        begin(0)

        @pl.when(low & jnp.logical_not(bwd.last))
        def _():
            bwd.serve(near, 0, False)

        w_y[0].wait()
        relay["y"][0].start()
        w_z[1].wait()
        relay["z"][1].start()
        w_z[2].wait()
        relay["z"][2].start()
        w_y[1].wait()
        relay["y"][1].start()
        grad_block(xp)
        for name in ("x", "z", "y"):
            wait(relay[name])
        grad_block(diag)

        @pl.when(bwd.first)
        def _():
            bwd.serve(far, 1, False)

        @pl.when(bwd.last)
        def _():
            bwd.serve(near, 0, False)

        for r in range(1, turns):
            begin(r)

        @pl.when(bwd.first)
        def _():
            bwd.send(far, 1)

        if piece != gcols:
            second_half()
            for r in range(turns):
                for j in range(width // 256):
                    acc = product(r, slice(j * 256, (j + 1) * 256))
                    for i in range(256 // piece):
                        spot = acc[:, i * piece : (i + 1) * piece]
                        part[j * (256 // piece) + i, spans[r], :] = spot.astype(BF)

                @pl.loop(0, m)
                def _(i):
                    to_y(r, i).start()

        each_block(far, grads_within)

        @pl.when(high & jnp.logical_not(bwd.first))
        def _():
            bwd.serve(far, 1)

        wide = width // 2

        @pl.loop(0, 2)
        def _(j):
            cols = pl.ds(pl.multiple_of(j * wide, wide), wide)
            mixed[:, cols] = dot(att[...], w_all[:, cols], 1, 0).astype(BF)

        @pl.when(low & jnp.logical_not(bwd.last))
        def _():
            bwd.serve(far, 1)

        if piece == gcols:
            second_half()

        def settle(r):
            @pl.loop(0, m)
            def _(i):
                to = hop(i)
                mine = to * 2 + yi
                if piece == gcols:
                    acc = product(r, cols_of(mine))
                else:
                    acc = part[mine, span(r), :].astype(F32)
                to_y(r, i).wait()
                acc = acc + pbox[to, span(r), :].astype(F32)
                part[mine, span(r), :] = acc.astype(BF)

                @pl.when(i < m - 1)
                def _():
                    to_z(r, i).start()

        settle(0)

        each_block(far, grads_query)

        @pl.when(bwd.last)
        def _():
            bwd.serve(far, 1)

        @pl.when(jnp.logical_not(bwd.first))
        def _():
            bwd.send(near, 0)

        for r in range(1, turns):
            settle(r)
        bwd.finish(far, 1)
        each_block(far, finals)
        bwd.finish(near, 0)
        each_block(near, finals)

        total = part[zi * 2 + yi].astype(F32)
        for i in range(m - 1):
            for r in range(turns):
                to_z(r, i).wait()
            total = total + zpart[i].astype(F32)
        wg[...] = total * grad_scale

    vmem = pltpu.VMEM
    sems = pltpu.SemaphoreType.DMA
    state = vmem((heads * HD, HD), BF)
    n_pat = 2 + 3 + NW + 4 * gcount + 3 * turns
    n_y = 2 + m * turns
    n_z = 3 + m * turns
    line = vmem((rows, width), BF)
    scratch = [
        line, line, line,
        vmem((width, width), BF),
        vmem((np_ * rows, width), BF),
        line,
        vmem((np_, rows, blk), BF),
        vmem((blk, np_ * rows), BF),
        vmem((heads, rows, rows), BF),
        vmem((heads, rows, rows), BF),
        vmem((rows, rows), F32),
        vmem((rows, width), BF),
        vmem((rows, width), F32),
        vmem((rows, width), F32),
        *[state] * 4,
        *[state] * 8,
        vmem((n, blk, piece), BF),
        vmem((m, blk, piece), BF),
        vmem((m, blk, piece), BF),
        sems((5,)),
        sems((n_pat,)), sems((n_pat,)),
        sems((n_y,)), sems((n_y,)),
        sems((n_z,)), sems((n_z,)),
        sems((2, 4 * NSC)), sems((2, 4 * NSC)),
    ]
    full = pltpu.VMEM((rows, width), BF)
    whole = pl.BlockSpec(memory_space=pltpu.VMEM)
    outside = pl.BlockSpec(memory_space=pltpu.HBM)
    grant = 54
    scalar = pl.BlockSpec(memory_space=pltpu.SMEM)
    return pl.pallas_call(
        kernel,
        out_shape=(full, full, full, full, pltpu.VMEM((blk, piece), F32)),
        in_specs=[outside] * 5 + [scalar] * 2,
        out_specs=(whole,) * 5,
        scratch_shapes=scratch,
        compiler_params=pltpu.CompilerParams(
            collective_id=0, has_side_effects=True, vmem_limit_bytes=grant * 1024 * 1024
        ),
    )


def hand_over(arrays):
    cuts = 2

    def kernel(*refs):
        n = len(arrays)
        src, dst, sem = refs[:n], refs[n : 2 * n], refs[2 * n]
        copies = []
        for i, a in enumerate(arrays):
            r = a.shape[0] // cuts
            for c in range(cuts):
                at = pl.ds(c * r, r)
                copies.append(pltpu.make_async_copy(src[i].at[at], dst[i].at[at], sem.at[i, c]))
        for copy in copies:
            copy.start()
        for copy in copies:
            copy.wait()

    anywhere = pl.BlockSpec(memory_space=pl.ANY)
    return pl.pallas_call(
        kernel,
        out_shape=tuple(jax.ShapeDtypeStruct(a.shape, a.dtype) for a in arrays),
        in_specs=[anywhere] * len(arrays),
        out_specs=(anywhere,) * len(arrays),
        scratch_shapes=[pltpu.SemaphoreType.DMA((len(arrays), cuts))],
        compiler_params=pltpu.CompilerParams(vmem_limit_bytes=1024 * 1024),
    )(*[pltpu.with_memory_space_constraint(a, pltpu.VMEM) for a in arrays])


def solution(mesh):
    n, np_ = mesh.shape["seq"], mesh.shape["pat"]

    def on_device(queries, key_rows, value_rows, out_weight, grad_out, visit_mask, lengths):
        rows, width = queries.shape[1:]
        call = make_kernel(
            n, np_, rows, width, visit_mask.shape[-1], 1.0 / math.sqrt(np_ * n * rows)
        )
        big = [queries[0], key_rows[0], value_rows[0], grad_out[0], out_weight]
        big = [pltpu.with_memory_space_constraint(a, pltpu.HBM) for a in big]
        mixed, dq, dk, dv, wg = call(*big, visit_mask, lengths)
        mixed, dq, dk, dv, wg = hand_over((mixed, dq, dk, dv, wg))
        return mixed[None], dq[None], dk[None], dv[None], wg

    rows3 = P("pat", "seq", None)
    return jax.shard_map(
        on_device,
        mesh=mesh,
        in_specs=(rows3, rows3, rows3, P("pat", None), rows3, P("pat", "seq", None, None), P("pat")),
        out_specs=(rows3, rows3, rows3, rows3, P("pat", "seq")),
        check_vma=False,
    )
```
